256 devices in a mesh: gx: 8 (over x, y_hi), gy: 16 (over y_lo, z), gz: 2 (over core).
Axes of the slice: x: 4, y: 4 (y_hi: 2, y_lo: 2; y = y_hi * 2 + y_lo), z: 8, core: 2. Of those that a mesh axis runs over, the one named last changes fastest.
Arguments:
- theta_field: float32 [8, 16, 128, 3072], P('gx', 'gy', 'gz'), may hold values from -6 to 6
- courants: bfloat16 [3, 8, 16, 128, 3072], P(None, 'gx', 'gy', 'gz'), may hold values from -0.27929688 to 0.27929688
- meso_columns: float32 [60, 262144], P(None, ('gx', 'gy', 'gz')), may hold values from -6 to 6
- col_weight: float32 [262144], P(('gx', 'gy', 'gz')), may hold values from 0.25 to 1
- owner_ids: int32 [262144, 1], P(('gx', 'gy', 'gz')), may hold values from 0 to 31; in each aligned block of 1024 rows (0 to 1023, 1024 to 2047, ...) at most 96 rows name the same one
- line_ids: int32 [262144], P(('gx', 'gy', 'gz')), may hold values from 0 to 191
- band_start: int32 [262144], P(('gx', 'gy', 'gz')), may hold values from 0 to 11
Outputs:
- theta_next: float32 [8, 16, 128, 3072], P('gx', 'gy', 'gz')
The draws below stay inside these ranges and needn't reach their ends.
Inputs may be any that keep to these rules, and one draw needn't show every extreme that they name: `owner_ids`: owner o is fringe side o mod 2 of y tile o div 2. Among the rows of one device no owner appears more than 96 times, and some owner appears exactly 96 times.
All inputs are finite; a program needn't handle non-finite values.
Results may differ from the reference program's by a relative error of at most 0.00059.
Values may be sent and summed in bfloat16 or wider, within the bound.
No kernel may reach another device: no remote copies, remote signals or barrier semaphores. Data moves between devices by JAX's collectives and lax.ppermute only.
A program may use at most 128 MiB of HBM per device.

```python
import math
import jax
import jax.numpy as jnp
import numpy as np
from jax import lax

CX = 16
NY = 3072
ZG = 128
LEV = 60
KM = 64
FW = 8
NSTEP = 4
COL_DEV = 1024
NX = 128
CY = 192
CAP = 96
COLS = 262144
N_GX = 8
N_GY = 16


def touch_ends(entries, own_key, low, largest):
    longest = entries.shape.index(max(entries.shape))
    spots = []
    for shift in (0, 1):
        where = [jax.random.randint(jax.random.fold_in(own_key, axis), (), 0, length) for axis, length in enumerate(entries.shape)]
        where[longest] = (where[longest] + shift) % entries.shape[longest]
        spots.append(tuple(where))
    return entries.at[spots[0]].set(low).at[spots[1]].set(largest)


def shard_levels(rng, extent, split, smallest, top_value):
    factor_of = 1.0
    for axis_at, shards_of in split:
        steps = jax.random.uniform(jax.random.fold_in(jax.random.fold_in(rng, 6), axis_at), (shards_of,), jnp.float32, smallest / len(split), top_value / len(split))
        factor_of = factor_of * jnp.repeat(jnp.exp(steps), extent[axis_at] // shards_of).reshape((-1,) + (1,) * (len(extent) - 1 - axis_at))
    return factor_of


def deal_out(rng, own, number, rows, number_of, top, limit, slope):
    ranking = jax.random.permutation(rng, number_of)
    crowded, usual = shares(number_of, rows * top, limit, slope, True), shares(number_of, rows * top, limit, slope, False)
    places = jnp.arange(number_of)

    def named(sizes, turn):
        used = int((sizes > 0).sum())
        fixed = max(1, used // 4)
        passed = fixed + (places - fixed + turn * (used - fixed)) % max(1, number_of - fixed)
        return jnp.zeros((number_of,), jnp.int32).at[ranking[jnp.where(places < fixed, places, passed)]].set(jnp.asarray(sizes, jnp.int32))

    sizes = jnp.where(number % 4 == 0, named(crowded, number // 4), named(usual, number - number // 4 - 1))
    mixed = jax.random.permutation(jax.random.fold_in(own, 3), number_of)
    source_of, receiver = mixed[0:number_of // 2 * 2:2], mixed[1:number_of // 2 * 2:2]
    margin = jnp.minimum(sizes[source_of] - 1, limit - sizes[receiver]) // 2
    margin = jnp.where((source_of == ranking[0]) | (receiver == ranking[0]) | (sizes[receiver] == 0), 0, jnp.maximum(margin, 0))
    passed = jax.random.randint(jax.random.fold_in(own, 4), (number_of // 2,), 0, 1 << 20) % (margin + 1)
    sizes = sizes.at[source_of].add(-passed).at[receiver].add(passed)
    members = jnp.searchsorted(jnp.cumsum(sizes), jnp.arange(rows * top), side="right").astype(jnp.int32)
    table = members.reshape(top, rows).T
    table = table[jax.random.permutation(jax.random.fold_in(own, 1), rows)]
    turn = jax.random.randint(jax.random.fold_in(own, 2), (rows, 1), 0, top)
    return jnp.take_along_axis(table, (jnp.arange(top)[None, :] + turn) % top, axis=1)


def shares(amount, total, most, lean, full):
    weights = [(1 << 20) // math.isqrt(standing ** lean) + 1 for standing in range(1, amount + 1)]
    largest = most if full else min(most, max(-(-total // amount), total * weights[0] // sum(weights)))
    least = 1 if total - largest >= amount - 1 else 0
    counts, surplus = [largest] + [least] * (amount - 1), total - largest - least * (amount - 1)
    while surplus > 0:
        movable = [i for i in range(1, amount) if counts[i] < largest] or [i for i in range(1, amount) if counts[i] < most]
        pool, remaining = sum([weights[i] for i in movable]), surplus
        for i in movable:
            extra = min(most - counts[i], max(1, remaining * weights[i] // pool), surplus)
            counts[i] = counts[i] + extra
            surplus = surplus - extra
    return np.array(counts)


def bell_draw(own_key, dims, width, limit, pieces=(), kind=jnp.bfloat16):
    array = width * jax.random.normal(own_key, dims, jnp.float32)
    if pieces:
        array = array * shard_levels(own_key, dims, pieces, -0.22, 0.18)
    return jnp.clip(array, -limit, limit).astype(kind)


def setup_inputs(seed: int = 0) -> dict:
    splits = jax.random.split(jax.random.key(seed), 8)
    theta_field = bell_draw(splits[0], (N_GX, N_GY, ZG, CX * CY), 1.0, 6.0, ((0, 8), (1, 16), (2, 2)), jnp.float32)
    courants = jnp.clip(jax.random.uniform(splits[1], (3, N_GX, N_GY, ZG, CX * CY), jnp.float32, -0.27929688, 0.27929688) * shard_levels(splits[1], (3, N_GX, N_GY, ZG, CX * CY), ((1, 8), (2, 16), (3, 2)), -0.4, 0.0), -0.27929688, 0.27929688).astype(jnp.bfloat16)
    meso_columns = bell_draw(splits[2], (LEV, COLS), 1.0, 6.0, ((1, 256),), jnp.float32)
    col_weight = jnp.clip(jnp.exp(math.log(1.0) - 1.3862944 * jax.random.uniform(splits[3], (COLS,), jnp.float32) ** shard_levels(splits[3], (COLS,), ((0, 256),), -0.2, 0.2)), 0.25, 1.0)
    owner_ids_keys = jax.random.split(jax.random.fold_in(splits[4], 1), COLS // COL_DEV)
    owner_ids_turns = jax.random.permutation(jax.random.fold_in(splits[4], 3), COLS // COL_DEV)
    owner_ids = jax.vmap(lambda own, number: deal_out(jax.random.fold_in(splits[4], 2), own, number, COL_DEV, 2 * N_GY, 1, CAP, 2))(owner_ids_keys, owner_ids_turns).reshape((COLS, 1))
    line_ids = touch_ends(jax.random.randint(splits[5], (COLS,), 0, CY), jax.random.fold_in(splits[5], 1), 0, CY - 1).astype(jnp.int32)
    band_start = touch_ends(jax.random.randint(splits[6], (COLS,), 0, LEV - 3 * (ZG - 1) // 8 - 1), jax.random.fold_in(splits[6], 1), 0, (LEV - 3 * (ZG - 1) // 8 - 1) - 1).astype(jnp.int32)
    return dict(theta_field=theta_field, courants=courants, meso_columns=meso_columns, col_weight=col_weight, owner_ids=owner_ids, line_ids=line_ids, band_start=band_start)


diffusion = 0.02


def band_lookup():
    levels_z = jnp.arange(ZG, dtype=jnp.int32)
    lower_index = (3 * levels_z) // 8
    fraction = ((3 * levels_z) % 8).astype(jnp.float32) / 8.0
    return lower_index, fraction


def wave_table(first_row, row_count):
    places = first_row + jnp.arange(row_count, dtype=jnp.int32)
    numbers = jnp.arange(KM, dtype=jnp.int32)
    phases = (places[:, None] * numbers[None, :]) % NY
    angles = phases.astype(jnp.float32) * (2.0 * math.pi / NY)
    return jnp.concatenate([jnp.cos(angles), jnp.sin(angles)], axis=1)


def mode_scale():
    return jnp.where(jnp.arange(2 * KM, dtype=jnp.int32) % KM == 0, 1.0 / NY, 2.0 / NY).astype(jnp.float32)


def upwind(state_field, courant_one, ahead_cell, behind_cell):
    return -jnp.maximum(courant_one, 0.0) * (state_field - behind_cell) - jnp.minimum(courant_one, 0.0) * (ahead_cell - state_field)


def advance(state_field, courants, ahead_x, behind_x, ahead_z, behind_z, ahead_y, behind_y):
    change = upwind(state_field, courants[0].astype(jnp.float32), ahead_x, behind_x)
    change = change + upwind(state_field, courants[1].astype(jnp.float32), ahead_z, behind_z)
    change = change + upwind(state_field, courants[2].astype(jnp.float32), ahead_y, behind_y)
    neighbours = ahead_x + behind_x + ahead_z + behind_z + ahead_y + behind_y
    return state_field + change + diffusion * (neighbours - 6.0 * state_field)


def sweep_once(state_field, courants):
    zero_layer = jnp.zeros_like(state_field[:, :1])
    ahead_z = jnp.concatenate([state_field[:, 1:], zero_layer], axis=1)
    behind_z = jnp.concatenate([zero_layer, state_field[:, :-1]], axis=1)
    return advance(state_field, courants, jnp.roll(state_field, -1, axis=0), jnp.roll(state_field, 1, axis=0), ahead_z, behind_z, jnp.roll(state_field, -1, axis=2), jnp.roll(state_field, 1, axis=2))


def to_grid(blocked):
    tiles_x = blocked.shape[0]
    tiles_y = blocked.shape[1]
    levels = blocked.shape[2]
    shaped = blocked.reshape(tiles_x, tiles_y, levels, CX, CY)
    return shaped.transpose(0, 3, 2, 1, 4).reshape(tiles_x * CX, levels, tiles_y * CY)


def to_blocks(grid):
    tiles_x = grid.shape[0] // CX
    tiles_y = grid.shape[2] // CY
    levels = grid.shape[1]
    shaped = grid.reshape(tiles_x, CX, levels, tiles_y, CY)
    return shaped.transpose(0, 3, 2, 1, 4).reshape(tiles_x, tiles_y, levels, CX * CY)


def reference(theta_field, courants, meso_columns, col_weight, owner_ids, line_ids, band_start):
    theta_grid = to_grid(theta_field)
    courant_grid = jnp.stack([to_grid(courants[0]), to_grid(courants[1]), to_grid(courants[2])])
    lower_index, fraction = band_lookup()
    column_major = meso_columns.T
    index_low = (band_start[:, None] + lower_index[None, :]).astype(jnp.int32)
    below_level = jnp.take_along_axis(column_major, index_low, axis=1)
    above_level = jnp.take_along_axis(column_major, index_low + 1, axis=1)
    profile = (1.0 - fraction)[None, :] * below_level + fraction[None, :] * above_level
    weighted = profile * col_weight[:, None]
    owners = owner_ids[:, 0]
    target_row = ((owners % 2) * NY + (owners // 2) * CY + line_ids).astype(jnp.int32)
    target = jax.ops.segment_sum(weighted, target_row, num_segments=2 * NY)
    target = target.reshape(2, NY, ZG).transpose(0, 2, 1)
    west_strip = theta_grid[:FW]
    east_strip = theta_grid[NX - FW:]
    gap_strip = jnp.concatenate([(target[0][None] - west_strip).astype(jnp.bfloat16), (target[1][None] - east_strip).astype(jnp.bfloat16)], axis=0)
    wave_basis = wave_table(0, NY)
    spectrum = jnp.einsum('xky,ym->xkm', gap_strip.astype(jnp.float32), wave_basis, precision=lax.Precision.HIGHEST)
    smooth = jnp.einsum('xkm,ym->xky', spectrum * mode_scale()[None, None, :], wave_basis, precision=lax.Precision.HIGHEST)
    offsets = jnp.arange(FW, dtype=jnp.float32)
    relax_west = (FW - offsets) / FW
    relax_east = (offsets + 1.0) / FW
    nudged = theta_grid.at[:FW].add(relax_west[:, None, None] * smooth[:FW])
    nudged = nudged.at[NX - FW:].add(relax_east[:, None, None] * smooth[FW:])
    state_field = nudged
    for step_index in range(NSTEP):
        state_field = sweep_once(state_field, courant_grid)
    return to_blocks(state_field)
```

```python
import math

import jax
import jax.numpy as jnp
from jax import lax
from jax.experimental import pallas as pl
from jax.experimental.pallas import tpu as pltpu
from jax.sharding import PartitionSpec as P

CX = 16
NY = 3072
ZG = 128
KM = 64
FW = 8
NSTEP = 4
HALO = 4
LZ = 64
CY = 192
RZ = 72
LANES = 256
XE = CX + 2 * HALO
DIFF = 0.02
XLANES = 768 + 3 * 640
YLANES = 384


def trig_table(rows, shape):
    modes = lax.broadcasted_iota(jnp.int32, shape, 0).astype(jnp.float32)
    phase = modes * rows
    phase = phase - NY * jnp.round(phase * (1.0 / NY))
    quarter = jnp.round(phase * (4.0 / NY))
    angle = (phase - quarter * (NY / 4)) * (2.0 * math.pi / NY)
    sq = angle * angle
    sin_p = angle * (
        1.0 + sq * (-1.0 / 6 + sq * (1.0 / 120 + sq * (-1.0 / 5040 + sq * (1.0 / 362880))))
    )
    cos_p = 1.0 + sq * (
        -0.5 + sq * (1.0 / 24 + sq * (-1.0 / 720 + sq * (1.0 / 40320 + sq * (-1.0 / 3628800))))
    )
    size = jnp.abs(quarter)
    odd = size == 1.0
    flip = jnp.where(size == 2.0, -1.0, 1.0)
    cos_v = jnp.where(odd, -quarter * sin_p, flip * cos_p)
    sin_v = jnp.where(odd, quarter * cos_p, flip * sin_p)
    return cos_v, sin_v


def dot3(a, b, dims):
    def parts(v):
        high = v.astype(jnp.bfloat16)
        return high, (v - high.astype(jnp.float32)).astype(jnp.bfloat16)
    a_high, a_low = parts(a)
    b_high, b_low = parts(b)
    def dot(x, y):
        return lax.dot_general(x, y, (dims, ((), ())), preferred_element_type=jnp.float32)
    return dot(a_high, b_high) + (dot(a_high, b_low) + dot(a_low, b_high))


def select(values, weights):
    high = values.astype(jnp.bfloat16)
    low = (values - high.astype(jnp.float32)).astype(jnp.bfloat16)
    weights = weights.astype(jnp.bfloat16)
    return jnp.dot(high, weights, preferred_element_type=jnp.float32) + jnp.dot(
        low, weights, preferred_element_type=jnp.float32
    )


def own_table(tile_index, masked):
    lane = lax.broadcasted_iota(jnp.int32, (KM, LANES), 1)
    cell = jnp.where(lane >= 224, lane - LANES, lane) + tile_index * CY
    cos_v, sin_v = trig_table(cell.astype(jnp.float32), (KM, LANES))
    table = jnp.concatenate([cos_v, sin_v], axis=0)
    if masked:
        keep = lax.broadcasted_iota(jnp.int32, (2 * KM, LANES), 1) < CY
        table = jnp.where(keep, table, 0.0)
    return table


def lane_id(rows):
    return lax.broadcasted_iota(jnp.int32, (rows, 128), 1)


def unpack_pair(t0, t1, t2):
    low = lane_id(t0.shape[0]) < 64
    r1 = pltpu.roll(t1, 64, 1)
    r2 = pltpu.roll(t2, 64, 1)
    return (t0, t1), (jnp.where(low, r1, r2), r2)


def partial_kernel(place, theta_hbm, cour_hbm, meso_hbm, weight_hbm, owner_hbm, line_hbm, start_hbm,
                   out_ref, tedge_ref, cedge_ref, right_ref, left_ref,
                   theta_ref, meso_ref, weight_ref, owner_ref, line_ref, start_ref,
                   cedge_buf, right_buf, left_buf, sems):
    at_east = place[3]
    half = place[2]
    base = pl.multiple_of(at_east * (FW * CY), 128)
    first = pl.multiple_of((1 - half) * (LZ - 8), 8)
    pairs = [
        (owner_hbm, owner_ref),
        (line_hbm, line_ref),
        (start_hbm, start_ref),
        (weight_hbm, weight_ref),
        (meso_hbm, meso_ref),
        (theta_hbm, theta_ref),
        (cour_hbm.at[:, pl.ds(first, 8)], cedge_buf),
        (cour_hbm.at[:, :, pl.ds(0, 640)], left_buf),
        (cour_hbm.at[:, :, pl.ds(CX * CY - 640, 640)], right_buf),
    ]
    copies = [
        pltpu.make_async_copy(source, target, sems.at[i])
        for i, (source, target) in enumerate(pairs)
    ]
    for copy in copies:
        copy.start()
    table = own_table(place[1], True)
    count = meso_ref.shape[1]
    for copy in copies[:4]:
        copy.wait()
    owner = owner_ref[...]
    side = jnp.bitwise_and(owner, 1)
    row = jnp.right_shift(owner, 1) * CY + line_ref[...]
    cos_v, sin_v = trig_table(
        jnp.broadcast_to(row.astype(jnp.float32), (KM, count)), (KM, count)
    )
    waves = jnp.concatenate([cos_v, sin_v], axis=0)
    start = jnp.broadcast_to(start_ref[...], (64, count))
    west = jnp.broadcast_to(side, (64, count)) == 0
    copies[4].wait()
    values = jnp.concatenate(
        [meso_ref[...], jnp.zeros((64 - meso_ref.shape[0], count), jnp.float32)], axis=0
    )
    for bit in (8, 4, 2, 1):
        values = jnp.where(
            jnp.bitwise_and(start, bit) != 0, pltpu.roll(values, 64 - bit, 0), values
        )
    values = values * weight_ref[...]
    sides = jnp.concatenate(
        [jnp.where(west, values, 0.0), jnp.where(west, 0.0, values)], axis=0
    )
    out_ref[:, 512:640] = dot3(waves, sides, ((1,), (1,)))
    copies[5].wait()
    for pair in range(FW // 2):
        tiles = [
            theta_ref[:, pl.ds(pl.multiple_of(base + pair * 384 + 128 * i, 128), 128)]
            for i in range(3)
        ]
        (a0, b0), (a1, b1) = unpack_pair(*tiles)
        block = jnp.concatenate(
            [jnp.concatenate([a0, b0], axis=1), jnp.concatenate([a1, b1], axis=1)], axis=0
        )
        out_ref[:, pair * 128 : (pair + 1) * 128] = dot3(table, block, ((1,), (1,)))
    tedge_ref[...] = theta_ref[pl.ds(first, 8), :]
    left_ref[:, 0:768] = theta_ref[:, 0:768].astype(jnp.bfloat16)
    right_ref[:, 0:768] = theta_ref[:, CX * CY - 768 :].astype(jnp.bfloat16)
    for copy in copies[6:]:
        copy.wait()
    cedge_ref[...] = cedge_buf[...]
    for d in range(3):
        left_ref[:, 768 + 640 * d : 1408 + 640 * d] = left_buf[d]
        right_ref[:, 768 + 640 * d : 1408 + 640 * d] = right_buf[d]


def share_kernel(place, got_ref, own_ref, send_ref):
    total = got_ref[0]
    for i in range(1, got_ref.shape[0]):
        total = total + got_ref[i]
    own_ref[...] = total[:, :512]
    at_east = place[3] == 1
    at_top = place[2] == 1
    source = lax.broadcasted_iota(jnp.int32, (512, 128), 0)
    target = lax.broadcasted_iota(jnp.int32, (512, 128), 1)
    slot = jnp.bitwise_and(target, 7)
    level = jnp.where(at_top, slot, slot + 56)
    valid = jnp.logical_xor(slot < 4, jnp.logical_not(at_top))
    pick = jnp.where(
        valid & (source == jnp.right_shift(target, 3) * 64 + level) & (target < 64), 1.0, 0.0
    )
    edge = select(total[:, :512], pick)
    strip = jnp.where(at_east, total[:, 256:512], total[:, 0:256])
    send = jnp.concatenate([strip, edge, total[:, 512:640]], axis=1)
    for i in range(send_ref.shape[0]):
        send_ref[i] = send


def gap_kernel(place, own_ref, got_ref, send_ref):
    count = got_ref.shape[0]
    total = got_ref[0][:, 384:512]
    for i in range(1, count):
        total = total + got_ref[i][:, 384:512]
    at_east = place[3]
    half = place[2]
    here = at_east * (count - 2)
    other = (1 - at_east) * (count - 2)
    lane = lax.broadcasted_iota(jnp.int32, (128, 896), 1)
    entry = lax.broadcasted_iota(jnp.int32, (128, 896), 0)
    slot = jnp.bitwise_and(lane, 7)
    in_edge = lane >= 768
    level = jnp.where(
        in_edge, jnp.where(slot < 4, slot + 64, slot - 8), jnp.bitwise_and(lane, 63)
    ) + half * LZ
    inside = (level >= 0) & (level < ZG)
    foreign = ((lane >= 512) & (lane < 768)) | (lane >= 832)
    side = jnp.where(foreign, 1 - at_east, at_east)
    lower = jnp.right_shift(3 * level, 3)
    fraction = jnp.bitwise_and(3 * level, 7).astype(jnp.float32) * 0.125
    index = entry - side * 64
    band = jnp.where(index == lower, 1.0 - fraction, jnp.where(index == lower + 1, fraction, 0.0))
    band = jnp.where(inside, band, 0.0)
    target = select(total, band)
    own_edge = got_ref[here + 1 - half][:, 256:384]
    other_edge = got_ref[other + 1 - half][:, 256:384]
    edges = jnp.where(lane_id(8) < 64, own_edge, pltpu.roll(other_edge, 64, 1))
    theta = jnp.concatenate([own_ref[...], got_ref[other + half][:, 0:256], edges], axis=1)
    gap = target - theta
    high = gap.astype(jnp.bfloat16)
    rest = (gap[:, 0:512] - high[:, 0:512].astype(jnp.float32)).astype(jnp.bfloat16)
    for i in range(send_ref.shape[0]):
        send_ref[i, :, 0:896] = high
        send_ref[i, :, 896:1408] = rest


def edge_pack_kernel(theta_hbm, cour_hbm, low_ref, high_ref, theta_ref, cour_ref, sems):
    copies = [
        pltpu.make_async_copy(theta_hbm, theta_ref, sems.at[0]),
        pltpu.make_async_copy(cour_hbm, cour_ref, sems.at[1]),
    ]
    for copy in copies:
        copy.start()
    for copy in copies:
        copy.wait()
    group = jnp.right_shift(lane_id(LZ), 2)

    def tile(field, i):
        cut = slice(128 * i, 128 * i + 128)
        return theta_ref[:, cut] if field == 0 else cour_ref[field - 1, :, cut].astype(jnp.float32)

    for block in range(2):
        low = jnp.zeros((LZ, 128), jnp.float32)
        high = jnp.zeros((LZ, 128), jnp.float32)
        for part in range(2):
            field = 2 * block + part
            tiles = [tile(field, i) for i in range(CX * CY // 128)]
            for x in range(CX):
                lo, hi = CY * x, CY * x + CY - HALO
                to = 64 * part + HALO * x
                mine = group == to // 4
                low = jnp.where(mine, pltpu.roll(tiles[lo // 128], (to - lo) % 128, 1), low)
                high = jnp.where(mine, pltpu.roll(tiles[hi // 128], (to - hi) % 128, 1), high)
        low_ref[:, 128 * block : 128 * block + 128] = low.astype(jnp.bfloat16)
        high_ref[:, 128 * block : 128 * block + 128] = high.astype(jnp.bfloat16)


def halo_level_kernel(place, xl_hbm, xr_hbm, yb_hbm, ya_hbm, out_ref, buf, sems):
    first = pl.multiple_of((1 - place[2]) * (LZ - 8), 8)
    copies = [
        pltpu.make_async_copy(source.at[pl.ds(first, 8)], buf.at[:, pl.ds(at, width)], sems.at[i])
        for i, (source, at, width) in enumerate((
            (xl_hbm, 0, XLANES), (xr_hbm, XLANES, XLANES),
            (yb_hbm, 2 * XLANES, YLANES), (ya_hbm, 2 * XLANES + YLANES, YLANES),
        ))
    ]
    for copy in copies:
        copy.start()
    for copy in copies:
        copy.wait()
    out_ref[...] = buf[...]


def corner_kernel(low_hbm, high_hbm, xl_ref, xr_ref, low_out, high_out, low_ref, high_ref, sems):
    copies = [
        pltpu.make_async_copy(source, target, sems.at[i])
        for i, (source, target) in enumerate((
            (low_hbm, low_ref), (high_hbm, high_ref),
        ))
    ]
    for copy in copies:
        copy.start()
    group = jnp.right_shift(lane_id(LZ), 2)
    edges = [jnp.zeros((LZ, 128), jnp.float32) for _ in range(2)]
    for field in range(4):
        base = 0 if field == 0 else 768 + 640 * (field - 1)
        width = 768 if field == 0 else 640
        for cell in range(2 * HALO):
            to = 32 * field + HALO * cell
            ref = xl_ref if cell < HALO else xr_ref
            first = CY * (cell % HALO)
            if cell < HALO:
                first = first - (768 - width)
            for which, lane in enumerate((first, first + CY - HALO)):
                if lane < 0 or lane >= width:
                    continue
                tile = ref[:, base + lane // 128 * 128 : base + lane // 128 * 128 + 128]
                moved = pltpu.roll(tile.astype(jnp.float32), (to - lane) % 128, 1)
                edges[which] = jnp.where(group == to // 4, moved, edges[which])
    for copy in copies:
        copy.wait()
    for out, ref, edge in ((low_out, low_ref, edges[0]), (high_out, high_ref, edges[1])):
        out[:, 0:256] = ref[...]
        out[:, 256:YLANES] = edge.astype(jnp.bfloat16)


def pack_pair(first, second):
    low = lane_id(first[0].shape[0]) < 64
    r1 = pltpu.roll(second[0], 64, 1)
    r2 = pltpu.roll(second[1], 64, 1)
    return first[0], jnp.where(low, first[1], r1), jnp.where(low, r1, r2)


def new_slab(coef, state, xi):
    lane = lane_id(RZ)
    t = [state[xi, :, 128 * w : 128 * w + 128] for w in range(2)]
    up = [pltpu.roll(v, 1, 1) for v in t]
    down = [pltpu.roll(v, 127, 1) for v in t]
    out = []
    for w in range(2):
        cut = slice(128 * w, 128 * w + 128)
        value = coef[6, xi, :, cut] * t[w]
        value = value + coef[0, xi, :, cut] * state[xi - 1, :, cut]
        value = value + coef[1, xi, :, cut] * state[xi + 1, :, cut]
        value = value + coef[2, xi, :, cut] * pltpu.roll(t[w], 1, 0)
        value = value + coef[3, xi, :, cut] * pltpu.roll(t[w], RZ - 1, 0)
        value = value + coef[4, xi, :, cut] * jnp.where(lane == 0, up[1 - w], up[w])
        value = value + coef[5, xi, :, cut] * jnp.where(lane == 127, down[1 - w], down[w])
        out.append(value)
    return out


def transport_kernel(place, spec_ref, theta_hbm, tz_hbm, cour_hbm, cz_hbm, xl_hbm, xr_hbm, yb_hbm, ya_hbm, hz_hbm,
                     out_hbm, theta_ref, tz_ref, cour_ref, cz_ref, xl_ref, xr_ref, yb_ref, ya_ref, hz_ref,
                     state_a, state_b, coef, smooth, out_ref, sems):
    half = place[2]
    at_east = place[3]
    at_west = place[4]
    lane = lane_id(RZ)
    copies = [
        pltpu.make_async_copy(source, target, sems.at[i])
        for i, (source, target) in enumerate((
            (hz_hbm, hz_ref), (cz_hbm, cz_ref), (yb_hbm, yb_ref), (ya_hbm, ya_ref),
            (xl_hbm, xl_ref), (xr_hbm, xr_ref), (cour_hbm, cour_ref),
            (tz_hbm, tz_ref), (theta_hbm, theta_ref),
        ))
    ]
    for copy in copies:
        copy.start()

    @pl.when(at_east + at_west > 0)
    def _():
        table = own_table(place[1], False)
        mode = lax.broadcasted_iota(jnp.int32, (2 * KM, LANES), 0)
        table = table * jnp.where(jnp.bitwise_and(mode, KM - 1) == 0, 1.0 / NY, 2.0 / NY)
        own = spec_ref[:, 0:512].astype(jnp.float32) + spec_ref[:, 896:1408].astype(jnp.float32)
        spectrum = jnp.concatenate([own, spec_ref[:, 512:896].astype(jnp.float32)], axis=1)
        spectrum = jnp.transpose(spectrum)
        smooth[...] = dot3(spectrum, table, ((1,), (0,)))

    for copy in copies[:7]:
        copy.wait()

    slot = lax.broadcasted_iota(jnp.int32, (8, 128), 0)
    inside = ((slot < 4) & (half == 0)) | ((slot >= 4) & (half == 1))
    keep_zed = jnp.where(inside, 1.0, 0.0)

    def tiles_of(field, pair):
        def read(ref, start, i, at=None):
            cut = slice(start + 128 * i, start + 128 * i + 128)
            value = ref[:, cut] if at is None else ref[at, :, cut]
            return value.astype(jnp.float32)
        if 2 <= pair < 10:
            at = None if field == 0 else field - 1
            refs = (theta_ref, tz_ref) if field == 0 else (cour_ref, cz_ref)
            own, zed = refs
            return [
                jnp.concatenate([read(own, 0, i, at), read(zed, 0, i, at) * keep_zed], axis=0)
                for i in range(3 * (pair - 2), 3 * (pair - 2) + 3)
            ]
        ref, zed = (xl_ref, 0) if pair < 2 else (xr_ref, XLANES)
        start = 0 if field == 0 else 768 + 640 * (field - 1)
        first = 3 * (pair if pair < 2 else pair - 10)
        wanted = [first + i for i in range(3)]
        if field > 0:
            wanted = [max(i - 1, 0) if pair < 2 else min(i, 4) for i in wanted]
        return [
            jnp.concatenate([read(ref, start, i), read(hz_ref, zed + start, i) * keep_zed], axis=0)
            for i in wanted
        ]

    def y_tiles(ref, at):
        return [
            jnp.concatenate([
                ref[:, 128 * i : 128 * i + 128].astype(jnp.float32),
                hz_ref[:, at + 128 * i : at + 128 * i + 128].astype(jnp.float32) * keep_zed,
            ], axis=0)
            for i in range(3)
        ]

    behind_tiles = y_tiles(yb_ref, 2 * XLANES)
    ahead_tiles = y_tiles(ya_ref, 2 * XLANES + YLANES)

    def with_halo(tile, field, xi):
        if HALO <= xi < HALO + CX:
            block, at = field // 2, 64 * (field % 2) + HALO * (xi - HALO)
        else:
            block, at = 2, 32 * field + HALO * (xi if xi < HALO else xi - CX)
        ra = pltpu.roll(ahead_tiles[block], (64 - at) % 128, 1)
        rb = pltpu.roll(behind_tiles[block], (124 - at) % 128, 1)
        return jnp.where(lane < 64, tile, jnp.where(lane < 96, ra, rb))

    keep = jnp.concatenate([jnp.ones((LZ, 128), jnp.float32), keep_zed], axis=0)
    base = keep * DIFF
    for pair in range(XE // 2):
        centre = [[keep] * 2 for _ in range(2)]
        for d in range(3):
            cells = unpack_pair(*tiles_of(d + 1, pair))
            for j in range(2):
                xi = 2 * pair + j
                if xi == 0 or xi == XE - 1:
                    continue
                parts = (cells[j][0], with_halo(cells[j][1], d + 1, xi))
                for w in range(2):
                    behind = jnp.maximum(parts[w], 0.0) + base
                    ahead = behind - parts[w]
                    coef[2 * d, xi, :, 128 * w : 128 * w + 128] = behind
                    coef[2 * d + 1, xi, :, 128 * w : 128 * w + 128] = ahead
                    centre[j][w] = centre[j][w] - (behind + ahead)
        for j in range(2):
            xi = 2 * pair + j
            if xi == 0 or xi == XE - 1:
                continue
            for w in range(2):
                coef[6, xi, :, 128 * w : 128 * w + 128] = centre[j][w]

    for copy in copies[7:]:
        copy.wait()
    for pair in range(XE // 2):
        cells = unpack_pair(*tiles_of(0, pair))
        for j in range(2):
            xi = 2 * pair + j
            state_a[xi, :, 0:128] = cells[j][0]
            state_a[xi, :, 128:256] = with_halo(cells[j][1], 0, xi)

    @pl.when(at_east + at_west > 0)
    def _():
        east = at_east.astype(jnp.float32)
        for i in range(FW):
            relax = east * ((i + 1.0) / FW) + (1.0 - east) * ((FW - i) / FW)
            xi = HALO + i + at_east * (CX - FW)
            state_a[xi, 0:64, :] += relax * smooth[64 * i : 64 * i + 64]
            state_a[xi, 64:72, :] += relax * smooth[768 + 8 * i : 776 + 8 * i]
        for i in range(HALO):
            relax = east * ((FW - i) / FW) + (1.0 - east) * ((HALO + i + 1.0) / FW)
            xi = i + at_east * (HALO + CX)
            state_a[xi, 0:64, :] += relax * smooth[512 + 64 * i : 576 + 64 * i]
            edge = jnp.where(
                at_east == 1, smooth[832 + 8 * i : 840 + 8 * i], smooth[864 + 8 * i : 872 + 8 * i]
            )
            state_a[xi, 64:72, :] += relax * edge

    def sweep(old, new, first, count):
        def one(xi):
            value = new_slab(coef, old, xi)
            for w in range(2):
                new[xi, :, 128 * w : 128 * w + 128] = value[w]

        def four(i, carry):
            for j in range(4):
                one(first + 4 * i + j)
            return carry

        lax.fori_loop(0, count // 4, four, 0)
        for j in range(count // 4 * 4, count):
            one(first + j)

    sweep(state_a, state_b, 1, XE - 2)
    sweep(state_b, state_a, 2, XE - 4)
    sweep(state_a, state_b, 3, XE - 6)

    outgoing = []
    for i in range(4):
        for j in range(2):
            x = 4 * i + 2 * j
            first = [v[0:64] for v in new_slab(coef, state_b, HALO + x)]
            second = [v[0:64] for v in new_slab(coef, state_b, HALO + x + 1)]
            for k, value in enumerate(pack_pair(first, second)):
                out_ref[:, x * CY + 128 * k : x * CY + 128 * k + 128] = value
        part = (slice(None), slice(768 * i, 768 * i + 768))
        copy = pltpu.make_async_copy(out_ref.at[part], out_hbm.at[part], sems.at[9 + i])
        copy.start()
        outgoing.append(copy)
    for copy in outgoing:
        copy.wait()


SMEM = pl.BlockSpec(memory_space=pltpu.SMEM)
VMEM = pl.BlockSpec(memory_space=pltpu.VMEM)
HBM = pl.BlockSpec(memory_space=pltpu.HBM)


def call(kernel, place, arrays, outs, scratch=(), mib=16, specs=VMEM, out_spec=VMEM, aliases=None):
    out_shape = [jax.ShapeDtypeStruct(s, d) for s, d in outs]
    single = len(outs) == 1
    inputs = ([] if place is None else [place]) + list(arrays)
    if not isinstance(specs, list):
        specs = [specs] * len(arrays)
    skip = len(inputs) - len(arrays)
    for i, spec in enumerate(specs):
        if spec is HBM:
            inputs[skip + i] = pltpu.with_memory_space_constraint(inputs[skip + i], pltpu.HBM)
    return pl.pallas_call(
        kernel,
        out_shape=out_shape[0] if single else out_shape,
        in_specs=([] if place is None else [SMEM]) + specs,
        out_specs=out_spec if single else [out_spec] * len(outs),
        scratch_shapes=list(scratch),
        input_output_aliases=aliases or {},
        compiler_params=pltpu.CompilerParams(vmem_limit_bytes=mib << 20),
    )(*inputs)


def body(theta_field, courants, meso_columns, col_weight, owner_ids, line_ids, band_start):
    f32, bf16 = jnp.float32, jnp.bfloat16
    n_gx = lax.axis_size("gx")
    n_gy = lax.axis_size("gy")
    gx, gy, gz = lax.axis_index("gx"), lax.axis_index("gy"), lax.axis_index("gz")
    place = jnp.stack(
        [gx, gy, gz, (gx == n_gx - 1).astype(jnp.int32), (gx == 0).astype(jnp.int32)]
    ).astype(jnp.int32)
    theta = theta_field.reshape(LZ, CX * CY)
    cour = courants.reshape(3, LZ, CX * CY)
    count = meso_columns.shape[1]

    swap = [(0, 1), (1, 0)]
    right = [(i, (i + 1) % n_gx) for i in range(n_gx)]
    left = [(j, i) for i, j in right]
    north = [(i, (i + 1) % n_gy) for i in range(n_gy)]
    south = [(j, i) for i, j in north]
    merged = CX * CY
    vmem, sems = pltpu.VMEM, pltpu.SemaphoreType.DMA
    partial, theta_edge, cour_edge, to_right, to_left = call(
        partial_kernel, place,
        [theta, cour, meso_columns, col_weight.reshape(1, count), owner_ids.reshape(1, count),
         line_ids.reshape(1, count), band_start.reshape(1, count)],
        [((2 * KM, 640), f32), ((8, merged), f32), ((3, 8, merged), bf16),
         ((LZ, XLANES), bf16), ((LZ, XLANES), bf16)],
        [vmem((LZ, merged), f32), vmem((meso_columns.shape[0], count), f32),
         vmem((1, count), f32)] + [vmem((1, count), jnp.int32)] * 3
        + [vmem((3, 8, merged), bf16), vmem((3, LZ, 640), bf16), vmem((3, LZ, 640), bf16), sems((9,))],
        specs=HBM,
    )
    modes = 2 * KM // n_gy
    got = lax.all_to_all(
        partial.reshape(n_gy, modes, 640), "gy", split_axis=0, concat_axis=0, tiled=True
    )

    xl = lax.ppermute(to_right, "gx", right)
    xr = lax.ppermute(to_left, "gx", left)
    tz = lax.ppermute(theta_edge, "gz", swap)
    cz = lax.ppermute(cour_edge, "gz", swap)
    low, high = call(
        edge_pack_kernel, None, [theta, cour],
        [((LZ, 256), bf16), ((LZ, 256), bf16)],
        [vmem((LZ, merged), f32), vmem((3, LZ, merged), bf16), sems((2,))],
        specs=HBM,
    )
    got, low, high = lax.optimization_barrier((got, low, high))

    ends = n_gx * 2
    own, send = call(share_kernel, place, [got], [((modes, 512), f32), ((ends, modes, 512), f32)])
    got = lax.all_to_all(send, ("gx", "gz"), split_axis=0, concat_axis=0, tiled=True)
    low, high = call(
        corner_kernel, None, [low, high, xl, xr], [((LZ, YLANES), bf16), ((LZ, YLANES), bf16)],
        [vmem((LZ, 256), bf16)] * 2 + [sems((2,))],
        mib=4, specs=[HBM, HBM, VMEM, VMEM],
    )
    yb = lax.ppermute(high, "gy", north)
    ya = lax.ppermute(low, "gy", south)
    got, yb, ya = lax.optimization_barrier((got, yb, ya))
    send = call(gap_kernel, place, [own, got], [((n_gy, modes, 1408), bf16)])
    halo_edge = call(
        halo_level_kernel, place, [xl, xr, yb, ya], [((8, 2 * XLANES + 2 * YLANES), bf16)],
        [vmem((8, 2 * XLANES + 2 * YLANES), bf16), sems((4,))], mib=4, specs=HBM,
    )
    hz = lax.ppermute(halo_edge, "gz", swap)
    spectrum = lax.all_to_all(send, "gy", split_axis=0, concat_axis=0, tiled=True)
    spectrum = spectrum.reshape(2 * KM, 1408)

    state = vmem((XE, RZ, LANES), f32)
    out = call(
        transport_kernel, place,
        [spectrum, theta, tz, cour, cz, xl, xr, yb, ya, hz],
        [((LZ, merged), f32)],
        [vmem((LZ, merged), f32), vmem((8, merged), f32), vmem((3, LZ, merged), bf16),
         vmem((3, 8, merged), bf16), vmem((LZ, XLANES), bf16), vmem((LZ, XLANES), bf16),
         vmem((LZ, YLANES), bf16), vmem((LZ, YLANES), bf16),
         vmem((8, 2 * XLANES + 2 * YLANES), bf16),
         state, state, vmem((7, XE, RZ, LANES), f32), vmem((896, LANES), f32), vmem((LZ, merged), f32), sems((13,))],
        mib=32, specs=[VMEM] + [HBM] * 9, out_spec=HBM,
    )
    return out.reshape(1, 1, LZ, merged)


def solution(mesh):
    in_specs = (
        P("gx", "gy", "gz", None),
        P(None, "gx", "gy", "gz", None),
        P(None, ("gx", "gy", "gz")),
        P(("gx", "gy", "gz")),
        P(("gx", "gy", "gz"), None),
        P(("gx", "gy", "gz")),
        P(("gx", "gy", "gz")),
    )
    out_specs = P("gx", "gy", "gz", None)
    return jax.shard_map(body, mesh=mesh, in_specs=in_specs, out_specs=out_specs, check_vma=False)
```
